32 devices in a mesh: section: 2 (over core), ep: 4 (over z), tp: 4 (over y, x).
Axes of the slice: x: 2, y: 2, z: 4, core: 2. Of those that a mesh axis runs over, the one named last changes fastest.
Arguments:
- hidden: bfloat16 [512, 6144], P('ep', ('section', 'tp')), may hold values from -6 to 6
- expert_ids: int32 [512, 2], P('ep'), may hold values from 0 to 7, all different within a row; in each aligned block of 128 rows (0 to 127, 128 to 255, ...) at most 40 rows name the same one
- gate_weights: float32 [512, 2], P('ep'), may hold values from 0 to 1, as said below
- gate_proj: bfloat16 [4, 6144, 16384], P('ep', None, ('section', 'tp')), may hold values from -0.078125 to 0.078125
- up_proj: bfloat16 [4, 6144, 16384], P('ep', None, ('section', 'tp')), may hold values from -0.078125 to 0.078125
- down_proj: bfloat16 [4, 6144, 16384], P('ep', ('section', 'tp')), may hold values from -0.0625 to 0.0625
Outputs:
- moe_out: bfloat16 [512, 6144], P('ep', ('section', 'tp'))
The draws below stay inside these ranges and needn't reach their ends.
Inputs may be any that keep to these rules, and one draw needn't show every extreme that they name: `expert_ids`: the two entries of a row differ. Within the 128 rows of one device no expert is named by more than 40 rows, and in some device's rows one expert is named by exactly 40. Every expert is named somewhere. `gate_weights`: the two weights of a token are positive, sum to one, and the first is at least the second.
All inputs are finite; a program needn't handle non-finite values.
Results may differ from the reference program's by a relative error of at most 0.0059.
Values may be sent and summed in bfloat16 or wider, within the bound.
A program may use at most 192 MiB of HBM per device.

```python
import math
import jax
import jax.numpy as jnp
import numpy as np
from jax import lax

D = 6144
E = 8
F = 8192
TOP = 2
TOK_DEV = 128
TOKENS = 512
CAP = 40
GCOLS = 16384
N_EP = 4


def draw_gate_weights(key, part):
    uniform_draw = jax.random.uniform(key, (TOKENS, 1), jnp.float32)
    leading = 0.5 + 0.45 * uniform_draw
    return jnp.concatenate([leading, 1.0 - leading], axis=1)


def block_levels(stream_key, dims, cuts, low, largest):
    loudness = 1.0
    for axis_at, shards_of in cuts:
        heights = jax.random.uniform(jax.random.fold_in(jax.random.fold_in(stream_key, 6), axis_at), (shards_of,), jnp.float32, low / len(cuts), largest / len(cuts))
        loudness = loudness * jnp.repeat(jnp.exp(heights), dims[axis_at] // shards_of).reshape((-1,) + (1,) * (len(dims) - 1 - axis_at))
    return loudness


def deal_out(own_key, own, number, rows, count, top, reach, slope):
    ranking = jax.random.permutation(own_key, count)
    heavy_load, common = load_shares(count, rows * top, reach, slope, True), load_shares(count, rows * top, reach, slope, False)
    places = jnp.arange(count)

    def named(lengths, offset_by):
        used = int((lengths > 0).sum())
        fixed = max(1, used // 4)
        passed = fixed + (places - fixed + offset_by * (used - fixed)) % max(1, count - fixed)
        return jnp.zeros((count,), jnp.int32).at[ranking[jnp.where(places < fixed, places, passed)]].set(jnp.asarray(lengths, jnp.int32))

    lengths = jnp.where(number % 4 == 0, named(heavy_load, number // 4), named(common, number - number // 4 - 1))
    mixed = jax.random.permutation(jax.random.fold_in(own, 3), count)
    source_of, taker = mixed[0:count // 2 * 2:2], mixed[1:count // 2 * 2:2]
    margin = jnp.minimum(lengths[source_of] - 1, reach - lengths[taker]) // 2
    margin = jnp.where((source_of == ranking[0]) | (taker == ranking[0]) | (lengths[taker] == 0), 0, jnp.maximum(margin, 0))
    passed = jax.random.randint(jax.random.fold_in(own, 4), (count // 2,), 0, 1 << 20) % (margin + 1)
    lengths = lengths.at[source_of].add(-passed).at[taker].add(passed)
    labels = jnp.searchsorted(jnp.cumsum(lengths), jnp.arange(rows * top), side="right").astype(jnp.int32)
    table = labels.reshape(top, rows).T
    table = table[jax.random.permutation(jax.random.fold_in(own, 1), rows)]
    offset_by = jax.random.randint(jax.random.fold_in(own, 2), (rows, 1), 0, top)
    return jnp.take_along_axis(table, (jnp.arange(top)[None, :] + offset_by) % top, axis=1)


def load_shares(number_of, total, most, skew, full):
    weights = [(1 << 20) // math.isqrt(standing ** skew) + 1 for standing in range(1, number_of + 1)]
    largest = most if full else min(most, max(-(-total // number_of), total * weights[0] // sum(weights)))
    least = 1 if total - largest >= number_of - 1 else 0
    holding, spare = [largest] + [least] * (number_of - 1), total - largest - least * (number_of - 1)
    while spare > 0:
        free = [i for i in range(1, number_of) if holding[i] < largest] or [i for i in range(1, number_of) if holding[i] < most]
        whole, remaining = sum([weights[i] for i in free]), spare
        for i in free:
            more = min(most - holding[i], max(1, remaining * weights[i] // whole), spare)
            holding[i] = holding[i] + more
            spare = spare - more
    return np.array(holding)


def noise(stream_key, shape, spread, limit, cuts=(), held_as=jnp.bfloat16):
    drawn = jax.random.normal(stream_key, shape, jnp.float32) * spread
    if len(cuts) > 0:
        drawn = block_levels(stream_key, shape, cuts, -0.22, 0.18) * drawn
    return jnp.clip(drawn, min=-limit, max=limit).astype(held_as)


def setup_inputs(seed: int = 0) -> dict:
    arg_keys = jax.random.split(jax.random.key(seed), 7)
    hidden = noise(arg_keys[0], (TOKENS, D), 1.0, 6.0, ((0, 4), (1, 8)))
    expert_ids_keys = jax.random.split(jax.random.fold_in(arg_keys[1], 1), TOKENS // TOK_DEV)
    expert_ids_turns = jax.random.permutation(jax.random.fold_in(arg_keys[1], 3), TOKENS // TOK_DEV)
    expert_ids = jax.vmap(lambda own, number: deal_out(jax.random.fold_in(arg_keys[1], 2), own, number, TOK_DEV, E, TOP, CAP, 1))(expert_ids_keys, expert_ids_turns).reshape((TOKENS, TOP))
    gate_weights = draw_gate_weights(jax.random.fold_in(arg_keys[6], 71), 0)
    gate_proj = noise(arg_keys[3], (N_EP, D, GCOLS), D ** -0.5, 0.078125, ((0, 4), (2, 8)))
    up_proj = noise(arg_keys[4], (N_EP, D, GCOLS), D ** -0.5, 0.078125, ((0, 4), (2, 8)))
    down_proj = noise(arg_keys[5], (N_EP, D, GCOLS), F ** -0.5, 0.0625, ((0, 4), (1, 8)))
    return {"hidden": hidden, "expert_ids": expert_ids, "gate_weights": gate_weights, "gate_proj": gate_proj, "up_proj": up_proj, "down_proj": down_proj}


def expert_columns(weight, expert):
    group_cols = weight.shape[2]
    if group_cols >= F:
        group_index = expert * F // group_cols
        offset = expert * F % group_cols
        return weight[group_index, :, offset:offset + F]
    block_count = F // group_cols
    blocks = weight[expert * block_count:(expert + 1) * block_count]
    return jnp.transpose(blocks, (1, 0, 2)).reshape(weight.shape[1], F)


def reference(hidden, expert_ids, gate_weights, gate_proj, up_proj, down_proj):
    bound_rows = N_EP * CAP
    block_cols = min(F, GCOLS)
    totals = jnp.zeros((TOKENS, D), jnp.float32)
    positions = jnp.arange(bound_rows).astype(jnp.int32)
    for expert in range(E):
        chosen = expert_ids == expert
        weights_here = jnp.sum(jnp.where(chosen, gate_weights, jnp.zeros_like(gate_weights)), axis=1)
        member = jnp.any(chosen, axis=1)
        picked = jnp.nonzero(member, size=bound_rows, fill_value=0)[0].astype(jnp.int32)
        live_count = jnp.sum(member.astype(jnp.int32))
        scaled = jnp.where(positions < live_count, weights_here[picked], jnp.zeros_like(weights_here[picked]))
        inputs = hidden[picked]
        gate_out = jnp.dot(inputs, expert_columns(gate_proj, expert), preferred_element_type=jnp.float32)
        up_out = jnp.dot(inputs, expert_columns(up_proj, expert), preferred_element_type=jnp.float32)
        activated = (jax.nn.silu(gate_out) * up_out).astype(jnp.bfloat16)
        down_cols = expert_columns(down_proj, expert)
        outputs = jnp.zeros((bound_rows, D), jnp.float32)
        for block in range(F // block_cols):
            low = block * block_cols
            part = lax.dot_general(activated[:, low:low + block_cols], down_cols[:, low:low + block_cols],
                                   (((1,), (1,)), ((), ())), preferred_element_type=jnp.float32)
            rounded = lax.optimization_barrier(part.astype(jnp.bfloat16))
            outputs = outputs + rounded.astype(jnp.float32)
        totals = totals.at[picked].add(scaled[:, None] * outputs)
    return totals.astype(jnp.bfloat16)
```

```python
import jax
import jax.numpy as jnp
from jax import lax
from jax.sharding import PartitionSpec as P

E = 8
F = 8192
CAP = 40


def slot_tables(expert_ids, capacity, experts):
    token_count = expert_ids.shape[0]
    flat_ids = expert_ids.reshape(-1)
    onehot = (flat_ids[:, None] == jnp.arange(experts, dtype=jnp.int32)[None, :]).astype(jnp.int32)
    before = jnp.cumsum(onehot, axis=0) - onehot
    position = jnp.sum(before * onehot, axis=1)
    slot_of = (flat_ids * capacity + position).reshape(token_count, -1)
    slot_range = jnp.arange(experts * capacity, dtype=jnp.int32)
    matches_st = slot_of[None, :, :] == slot_range[:, None, None]
    dispatch = jnp.any(matches_st, axis=2).astype(jnp.bfloat16)
    return (dispatch, slot_of)


def on_device(hidden, expert_ids, gate_weights, gate_proj, up_proj, down_proj):
    ep_count = lax.axis_size("ep")
    share_count = lax.axis_size("section") * lax.axis_size("tp")
    owners_each = max(1, ep_count // E)
    experts_each = max(1, E // ep_count)
    local_cols = gate_proj.shape[2]
    group_cols = local_cols * share_count
    owner_index = lax.axis_index("ep")
    share_index = lax.axis_index("section") * lax.axis_size("tp") + lax.axis_index("tp")
    own_expert = (owner_index * group_cols + share_index * local_cols) // F
    slot_expert = owner_index // owners_each * experts_each + jnp.arange(
        experts_each, dtype=jnp.int32
    )
    keep_mask = (slot_expert == own_expert).reshape(1, experts_each, 1, 1)
    gate_local = gate_proj[0]
    up_local = up_proj[0]
    down_local = down_proj[0]
    dispatch, slot_of = slot_tables(expert_ids, CAP, E)
    packed = jnp.dot(
        dispatch,
        lax.all_gather(hidden, ("section", "tp"), axis=1, tiled=True),
        preferred_element_type=jnp.float32,
    ).astype(jnp.bfloat16)
    grouped = packed.reshape(E // experts_each, experts_each, CAP, packed.shape[1])
    received = lax.all_to_all(
        jnp.repeat(grouped, owners_each, axis=0), "ep", split_axis=0, concat_axis=0, tiled=True
    )
    flat_rows = received.reshape(-1, received.shape[3])
    gate_out = jnp.dot(flat_rows, gate_local, preferred_element_type=jnp.float32)
    up_out = jnp.dot(flat_rows, up_local, preferred_element_type=jnp.float32)
    lead_shape = received.shape[:3]
    activated = (jax.nn.silu(gate_out) * up_out).reshape(lead_shape + (local_cols,))
    activated = jnp.where(keep_mask, activated, 0.0).astype(jnp.bfloat16)
    flat_act = activated.reshape(-1, local_cols)
    outputs = lax.dot_general(
        lax.all_gather(flat_act, ("section", "tp"), axis=1, tiled=True),
        down_local,
        (((1,), (1,)), ((), ())),
        preferred_element_type=jnp.float32,
    )
    outputs = outputs.reshape(lead_shape + (down_local.shape[0],)).astype(jnp.bfloat16)
    returned = lax.all_to_all(outputs, "ep", split_axis=0, concat_axis=0, tiled=True)
    grouped = returned.astype(jnp.float32).reshape(
        E // experts_each, owners_each, experts_each, CAP, returned.shape[3]
    )
    summed = jnp.sum(grouped, axis=1).reshape(E * CAP, returned.shape[3])
    first_rows = summed[slot_of[:, 0]]
    second_rows = summed[slot_of[:, 1]]
    combined_out = gate_weights[:, 0:1] * first_rows + gate_weights[:, 1:2] * second_rows
    return combined_out.astype(jnp.bfloat16)


def on_device_paired(hidden, expert_ids, gate_weights, gate_proj, up_proj, down_proj):
    ep_count = lax.axis_size("ep")
    pair = lax.axis_size("section")
    width = hidden.shape[1]
    local_cols = gate_proj.shape[2]
    dispatch, slot_of = slot_tables(expert_ids, CAP, E)
    packed = jnp.dot(dispatch, hidden, preferred_element_type=jnp.float32).astype(jnp.bfloat16)
    sent = packed.reshape(ep_count, pair, CAP, width)
    received = lax.all_to_all(sent, "ep", split_axis=0, concat_axis=0, tiled=True)
    swapped = lax.all_to_all(received, "section", split_axis=1, concat_axis=1, tiled=True)
    halves = lax.all_gather(swapped, "tp", axis=0)
    rows = jnp.transpose(halves, (1, 3, 2, 0, 4)).reshape(ep_count * CAP, -1)
    gate_out = jnp.dot(rows, gate_proj[0], preferred_element_type=jnp.float32)
    up_out = jnp.dot(rows, up_proj[0], preferred_element_type=jnp.float32)
    activated = (jax.nn.silu(gate_out) * up_out).astype(jnp.bfloat16)
    gathered = lax.all_gather(activated, "tp", axis=1, tiled=True)
    both = lax.all_gather(gathered, "section", axis=0)
    outputs = jnp.stack(
        [
            lax.dot_general(
                both[i], down_proj[0][:, i * F : (i + 1) * F], (((1,), (1,)), ((), ())),
                preferred_element_type=jnp.float32,
            ).astype(jnp.bfloat16).reshape(ep_count, CAP, width)
            for i in range(pair)
        ],
        axis=1,
    )
    returned = lax.all_to_all(outputs, "ep", split_axis=0, concat_axis=0, tiled=True)
    flat = returned.reshape(E * CAP, width)
    slot_range = jnp.arange(E * CAP, dtype=jnp.int32)[None, :]
    picks = [(slot_of[:, k : k + 1] == slot_range).astype(jnp.bfloat16) for k in range(2)]
    first_rows, second_rows = [jnp.dot(p, flat, preferred_element_type=jnp.float32) for p in picks]
    combined = gate_weights[:, 0:1] * first_rows + gate_weights[:, 1:2] * second_rows
    return combined.astype(jnp.bfloat16)


def solution(mesh):
    def body(*args):
        paired = E // mesh.shape["ep"] == mesh.shape["section"] and args[3].shape[2] * mesh.shape["tp"] == F
        return (on_device_paired if paired else on_device)(*args)

    return jax.shard_map(
        body,
        mesh=mesh,
        in_specs=(
            P("ep", ("section", "tp")),
            P("ep", None),
            P("ep", None),
            P("ep", None, ("section", "tp")),
            P("ep", None, ("section", "tp")),
            P("ep", ("section", "tp"), None),
        ),
        out_specs=P("ep", ("section", "tp")),
        check_vma=False,
    )
```

```python
import jax
import jax.numpy as jnp
from jax import lax
from jax.experimental import pallas as pl
from jax.experimental.pallas import tpu as pltpu
from jax.sharding import PartitionSpec as P

E = 8
F = 8192
CAP = 40


def slot_tables(expert_ids, capacity, experts):
    token_count = expert_ids.shape[0]
    flat_ids = expert_ids.reshape(-1)
    onehot = (flat_ids[:, None] == jnp.arange(experts, dtype=jnp.int32)[None, :]).astype(jnp.int32)
    before = jnp.cumsum(onehot, axis=0) - onehot
    position = jnp.sum(before * onehot, axis=1)
    slot_of = (flat_ids * capacity + position).reshape(token_count, -1)
    slot_range = jnp.arange(experts * capacity, dtype=jnp.int32)
    matches_st = slot_of[None, :, :] == slot_range[:, None, None]
    dispatch = jnp.any(matches_st, axis=2).astype(jnp.bfloat16)
    return (dispatch, slot_of)


def on_device(hidden, expert_ids, gate_weights, gate_proj, up_proj, down_proj):
    ep_count = lax.axis_size("ep")
    share_count = lax.axis_size("section") * lax.axis_size("tp")
    owners_each = max(1, ep_count // E)
    experts_each = max(1, E // ep_count)
    local_cols = gate_proj.shape[2]
    group_cols = local_cols * share_count
    owner_index = lax.axis_index("ep")
    share_index = lax.axis_index("section") * lax.axis_size("tp") + lax.axis_index("tp")
    own_expert = (owner_index * group_cols + share_index * local_cols) // F
    slot_expert = owner_index // owners_each * experts_each + jnp.arange(
        experts_each, dtype=jnp.int32
    )
    keep_mask = (slot_expert == own_expert).reshape(1, experts_each, 1, 1)
    gate_local = gate_proj[0]
    up_local = up_proj[0]
    down_local = down_proj[0]
    dispatch, slot_of = slot_tables(expert_ids, CAP, E)
    packed = jnp.dot(
        dispatch,
        lax.all_gather(hidden, ("section", "tp"), axis=1, tiled=True),
        preferred_element_type=jnp.float32,
    ).astype(jnp.bfloat16)
    grouped = packed.reshape(E // experts_each, experts_each, CAP, packed.shape[1])
    received = lax.all_to_all(
        jnp.repeat(grouped, owners_each, axis=0), "ep", split_axis=0, concat_axis=0, tiled=True
    )
    flat_rows = received.reshape(-1, received.shape[3])
    gate_out = jnp.dot(flat_rows, gate_local, preferred_element_type=jnp.float32)
    up_out = jnp.dot(flat_rows, up_local, preferred_element_type=jnp.float32)
    lead_shape = received.shape[:3]
    activated = (jax.nn.silu(gate_out) * up_out).reshape(lead_shape + (local_cols,))
    activated = jnp.where(keep_mask, activated, 0.0).astype(jnp.bfloat16)
    flat_act = activated.reshape(-1, local_cols)
    outputs = lax.dot_general(
        lax.all_gather(flat_act, ("section", "tp"), axis=1, tiled=True),
        down_local,
        (((1,), (1,)), ((), ())),
        preferred_element_type=jnp.float32,
    )
    outputs = outputs.reshape(lead_shape + (down_local.shape[0],)).astype(jnp.bfloat16)
    returned = lax.all_to_all(outputs, "ep", split_axis=0, concat_axis=0, tiled=True)
    grouped = returned.astype(jnp.float32).reshape(
        E // experts_each, owners_each, experts_each, CAP, returned.shape[3]
    )
    summed = jnp.sum(grouped, axis=1).reshape(E * CAP, returned.shape[3])
    first_rows = summed[slot_of[:, 0]]
    second_rows = summed[slot_of[:, 1]]
    combined_out = gate_weights[:, 0:1] * first_rows + gate_weights[:, 1:2] * second_rows
    return combined_out.astype(jnp.bfloat16)

SLOTS = 10
PARTS = 3
CHUNKS = 4
MESH = pl.DeviceIdType.MESH


def layer_kernel(
    hidden_ref, dispatch_ref, picks_ref, weights_ref, gate_ref, up_ref, down_ref, out_ref,
    sent, landed, across, x_all, w_buf, d_buf, acc, act_all, totals, back, ret,
    z_send, z_recv, s_send, s_recv, x_send, x_recv, a_send, a_recv, c_send, c_recv, r_send, r_recv, w_sem, d_sem,
):
    width = hidden_ref.shape[1]
    part = width // PARTS
    rows = 4 * CAP
    half = rows // 2
    units = 2 * PARTS
    cols = gate_ref.shape[2]
    chunk = cols // CHUNKS
    steps = 4 * units
    section = lax.axis_index("section")
    z = lax.axis_index("ep")
    tp = lax.axis_index("tp")
    tx, ty = tp % 2, tp // 2
    other = 1 - section

    def place(rel):
        return (ty + rel // 2) % 2 * 2 + (tx + rel % 2) % 2

    x_near, y_near, far = place(1), place(2), place(3)

    def weight_copies(step):
        rel, unit = step // units, step % units
        core = (section + unit % 2) % 2
        row = pl.multiple_of(((core * 4 + place(rel)) * PARTS + unit // 2) * part, part)
        slot = step % SLOTS
        return [
            pltpu.make_async_copy(ref.at[0, pl.ds(row, part), :], w_buf.at[slot, i], w_sem.at[slot, i])
            for i, ref in enumerate((gate_ref, up_ref))
        ]

    def down_copy(index):
        at = pl.multiple_of(index * chunk, chunk)
        return pltpu.make_async_copy(down_ref.at[0, :, pl.ds(at, chunk)], d_buf.at[index], d_sem.at[index])

    @pl.loop(0, SLOTS)
    def _(step):
        for copy in weight_copies(step):
            copy.start()

    @pl.loop(0, 8 * CHUNKS)
    def _(index):
        down_copy(index).start()

    barrier = pltpu.get_barrier_semaphore()
    for d in range(1, 4):
        pl.semaphore_signal(barrier, inc=1, device_id={"ep": (z + d) % 4}, device_id_type=MESH)
    pl.semaphore_signal(barrier, inc=1, device_id={"section": other}, device_id_type=MESH)
    pl.semaphore_signal(barrier, inc=1, device_id={"tp": x_near}, device_id_type=MESH)
    pl.semaphore_signal(barrier, inc=1, device_id={"tp": y_near}, device_id_type=MESH)

    packed = jnp.dot(dispatch_ref[...], hidden_ref[...], preferred_element_type=jnp.float32)
    packed = packed.astype(jnp.bfloat16)
    for g in range(4):
        for h in range(PARTS):
            sent[g, h] = packed[g * 2 * CAP : (g + 1) * 2 * CAP, h * part : (h + 1) * part]
    pl.semaphore_wait(barrier, 6)

    def remote(src, dst, send, recv, target):
        return pltpu.make_async_remote_copy(
            src_ref=src, dst_ref=dst, send_sem=send, recv_sem=recv, device_id=target, device_id_type=MESH
        )

    def z_copy(h, d):
        g = (z + d) % 4
        return remote(sent.at[g, h], landed.at[z, h], z_send.at[h, g], z_recv.at[h, z], {"ep": g})

    def z_arrival(h, d):
        g = (z + d) % 4
        return remote(sent.at[g, h], landed.at[g, h], z_send.at[h, g], z_recv.at[h, g], {"ep": g})

    @pl.loop(0, PARTS)
    def _(h):
        for d in (2, 1, 3):
            z_copy(h, d).start()

    for h in range(PARTS):
        landed[z, h] = sent[z, h]
    acc[...] = jnp.zeros_like(acc)
    totals[...] = jnp.zeros_like(totals)

    def spread(buf, at, send, recv, kind, unit):
        if kind < 2:
            index, target = at(tp, unit), {"tp": (x_near, y_near)[kind]}
            ref = buf.at[index]
        else:
            index, target = at((x_near, y_near)[kind - 2], unit), {"tp": (y_near, x_near)[kind - 2]}
            ref = buf.at[index, pl.ds((half, 0)[kind - 2], half), :]
        return remote(ref, ref, send.at[kind, unit], recv.at[kind, unit], target)

    def arrival(buf, at, send, recv, kind, unit):
        if kind < 2:
            ref = buf.at[at((x_near, y_near)[kind], unit)]
        else:
            ref = buf.at[at(far, unit), pl.ds((half, 0)[kind - 2], half), :]
        return remote(ref, ref, send.at[kind, unit], recv.at[kind, unit], {"tp": (x_near, y_near, y_near, x_near)[kind]})

    def x_at(place_of, unit):
        return place_of * units + unit

    x_args = (x_all, x_at, x_send, x_recv)

    def swap_copy(h):
        return remote(
            across.at[h], x_all.at[x_at(tp, 2 * h + 1)], s_send.at[h], s_recv.at[h], {"section": other}
        )

    @pl.loop(0, PARTS)
    def _(h):
        for d in (1, 3, 2):
            z_arrival(h, d).wait_recv()
        blocks = [landed[g, h].astype(jnp.float32) for g in range(4)]
        first = jnp.concatenate([b[:CAP] for b in blocks], axis=0)
        second = jnp.concatenate([b[CAP:] for b in blocks], axis=0)
        across[h] = jnp.where(section == 0, second, first).astype(jnp.bfloat16)
        swap_copy(h).start()
        x_all[x_at(tp, 2 * h)] = jnp.where(section == 0, first, second).astype(jnp.bfloat16)
        spread(*x_args, 0, 2 * h).start()
        spread(*x_args, 1, 2 * h).start()
        swap_copy(h).wait_recv()
        spread(*x_args, 0, 2 * h + 1).start()
        spread(*x_args, 1, 2 * h + 1).start()

    def gate_step(rel, unit):
        step = rel * units + unit
        slot = step % SLOTS
        for copy in weight_copies(step):
            copy.wait()
        x = x_all[x_at(place(rel), unit)]
        for i in range(2):
            for j in range(CHUNKS):
                acc[i, j] += jnp.dot(
                    x, w_buf[slot, i, :, j * chunk : (j + 1) * chunk], preferred_element_type=jnp.float32
                )

        @pl.when(step + SLOTS < steps)
        def _():
            for copy in weight_copies(step + SLOTS):
                copy.start()

    @pl.loop(0, units)
    def _(unit):
        gate_step(0, unit)
        for kind in range(2):
            arrival(*x_args, kind, unit).wait_recv()
            spread(*x_args, kind + 2, unit).start()

    @pl.loop(0, 2 * units)
    def _(k):
        gate_step(1 + k // units, k % units)

    @pl.loop(0, units)
    def _(unit):
        for kind in (2, 3):
            arrival(*x_args, kind, unit).wait_recv()
        gate_step(3, unit)

    def act_at(place_of, j, core=None):
        return ((section if core is None else core) * 4 + place_of) * CHUNKS + j

    a_args = (act_all, act_at, a_send, a_recv)

    def cross_copy(rel, j):
        ref = act_all.at[act_at(place(rel), j)]
        return remote(ref, ref, c_send.at[rel, j], c_recv.at[rel, j], {"section": other})

    def cross_arrival(rel, j):
        ref = act_all.at[act_at(place(rel), j, other)]
        return remote(ref, ref, c_send.at[rel, j], c_recv.at[rel, j], {"section": other})

    def down_step(core, rel, j):
        index = act_at(place(rel), j, core)
        down_copy(index).wait()
        totals[core] += lax.dot_general(
            act_all[index], d_buf[index], (((1,), (1,)), ((), ())), preferred_element_type=jnp.float32
        )

    @pl.loop(0, CHUNKS)
    def _(j):
        gate_out = acc[0, j]
        act_all[act_at(tp, j)] = (gate_out / (1.0 + jnp.exp(-gate_out)) * acc[1, j]).astype(jnp.bfloat16)
        spread(*a_args, 0, j).start()
        spread(*a_args, 1, j).start()
        cross_copy(0, j).start()

    @pl.loop(0, CHUNKS)
    def _(j):
        down_step(section, 0, j)
        cross_arrival(0, j).wait_recv()
        down_step(other, 0, j)
        for kind in range(2):
            arrival(*a_args, kind, j).wait_recv()
            spread(*a_args, kind + 2, j).start()
            cross_copy(kind + 1, j).start()

    @pl.loop(0, CHUNKS)
    def _(j):
        down_step(section, 1, j)
        down_step(section, 2, j)
        for kind in (2, 3):
            arrival(*a_args, kind, j).wait_recv()
        cross_copy(3, j).start()
        for rel in (1, 2):
            cross_arrival(rel, j).wait_recv()
            down_step(other, rel, j)
        down_step(section, 3, j)

    @pl.loop(0, CHUNKS)
    def _(j):
        cross_arrival(3, j).wait_recv()
        down_step(other, 3, j)

    def back_copy(d):
        g = (z + d) % 4
        return remote(back.at[g], ret.at[z], r_send.at[g], r_recv.at[z], {"ep": g})

    def back_arrival(d):
        g = (z + d) % 4
        return remote(back.at[g], ret.at[g], r_send.at[g], r_recv.at[g], {"ep": g})

    for g in range(4):
        back[g] = jnp.concatenate(
            [totals[e, g * CAP : (g + 1) * CAP, :] for e in range(2)], axis=0
        ).astype(jnp.bfloat16)
    for d in (2, 1, 3):
        back_copy(d).start()
    ret[z] = back[z]
    for d in (1, 3, 2):
        back_arrival(d).wait_recv()
    both = jnp.dot(
        picks_ref[...], ret[...].reshape(8 * CAP, width), preferred_element_type=jnp.float32
    )
    tokens = hidden_ref.shape[0]
    combined = weights_ref[:, 0:1] * both[:tokens] + weights_ref[:, 1:2] * both[tokens:]
    out_ref[...] = combined.astype(out_ref.dtype)

    for d in range(1, 4):
        back_copy(d).wait_send()

    @pl.loop(0, PARTS)
    def _(h):
        for d in range(1, 4):
            z_copy(h, d).wait_send()
        swap_copy(h).wait_send()

    @pl.loop(0, units)
    def _(unit):
        for kind in range(4):
            spread(*x_args, kind, unit).wait_send()

    @pl.loop(0, CHUNKS)
    def _(j):
        for kind in range(4):
            spread(*a_args, kind, j).wait_send()
        for rel in range(4):
            cross_copy(rel, j).wait_send()


def on_device_paired(hidden, expert_ids, gate_weights, gate_proj, up_proj, down_proj):
    tokens, width = hidden.shape
    cols = gate_proj.shape[2]
    part, chunk, rows = width // PARTS, cols // CHUNKS, 4 * CAP
    dispatch, slot_of = slot_tables(expert_ids, CAP, E)
    slot_range = jnp.arange(E * CAP, dtype=jnp.int32)[None, :]
    picks = (slot_of.T.reshape(-1, 1) == slot_range).astype(jnp.bfloat16)
    vmem = pl.BlockSpec(memory_space=pltpu.VMEM)
    anywhere = pl.BlockSpec(memory_space=pl.ANY)
    sem = pltpu.SemaphoreType.DMA
    return pl.pallas_call(
        layer_kernel,
        out_shape=jax.ShapeDtypeStruct((tokens, width), jnp.bfloat16),
        in_specs=[vmem] * 4 + [anywhere] * 3,
        out_specs=vmem,
        scratch_shapes=[
            pltpu.VMEM((4, PARTS, 2 * CAP, part), jnp.bfloat16),
            pltpu.VMEM((4, PARTS, 2 * CAP, part), jnp.bfloat16),
            pltpu.VMEM((PARTS, rows, part), jnp.bfloat16),
            pltpu.VMEM((8 * PARTS, rows, part), jnp.bfloat16),
            pltpu.VMEM((SLOTS, 2, part, cols), jnp.bfloat16),
            pltpu.VMEM((8 * CHUNKS, width, chunk), jnp.bfloat16),
            pltpu.VMEM((2, CHUNKS, rows, chunk), jnp.float32),
            pltpu.VMEM((8 * CHUNKS, rows, chunk), jnp.bfloat16),
            pltpu.VMEM((2, rows, width), jnp.float32),
            pltpu.VMEM((4, 2 * CAP, width), jnp.bfloat16),
            pltpu.VMEM((4, 2 * CAP, width), jnp.bfloat16),
            sem((PARTS, 4)), sem((PARTS, 4)), sem((PARTS,)), sem((PARTS,)),
            sem((4, 2 * PARTS)), sem((4, 2 * PARTS)), sem((4, CHUNKS)), sem((4, CHUNKS)),
            sem((4, CHUNKS)), sem((4, CHUNKS)), sem((4,)), sem((4,)),
            sem((SLOTS, 2)), sem((8 * CHUNKS,)),
        ],
        compiler_params=pltpu.CompilerParams(
            collective_id=0, has_side_effects=True, vmem_limit_bytes=62 * 1024 * 1024
        ),
    )(hidden, dispatch, picks, gate_weights, gate_proj, up_proj, down_proj)


def solution(mesh):
    def body(*args):
        paired = mesh.shape["ep"] == 4 and mesh.shape["section"] == 2 and mesh.shape["tp"] == 4
        paired = paired and E // mesh.shape["ep"] == mesh.shape["section"] and args[3].shape[2] * mesh.shape["tp"] == F
        return (on_device_paired if paired else on_device)(*args)

    return jax.shard_map(
        body,
        mesh=mesh,
        in_specs=(
            P("ep", ("section", "tp")),
            P("ep", None),
            P("ep", None),
            P("ep", None, ("section", "tp")),
            P("ep", None, ("section", "tp")),
            P("ep", ("section", "tp"), None),
        ),
        out_specs=P("ep", ("section", "tp")),
        check_vma=False,
    )
```

```python
import jax
import jax.numpy as jnp
from jax import lax
from jax.experimental import pallas as pl
from jax.experimental.pallas import tpu as pltpu
from jax.sharding import PartitionSpec as P

E = 8
F = 8192
CAP = 40


def slot_tables(expert_ids, capacity, experts):
    token_count = expert_ids.shape[0]
    flat_ids = expert_ids.reshape(-1)
    onehot = (flat_ids[:, None] == jnp.arange(experts, dtype=jnp.int32)[None, :]).astype(jnp.int32)
    before = jnp.cumsum(onehot, axis=0) - onehot
    position = jnp.sum(before * onehot, axis=1)
    slot_of = (flat_ids * capacity + position).reshape(token_count, -1)
    slot_range = jnp.arange(experts * capacity, dtype=jnp.int32)
    matches_st = slot_of[None, :, :] == slot_range[:, None, None]
    dispatch = jnp.any(matches_st, axis=2).astype(jnp.bfloat16)
    return (dispatch, slot_of)


def on_device(hidden, expert_ids, gate_weights, gate_proj, up_proj, down_proj):
    ep_count = lax.axis_size("ep")
    share_count = lax.axis_size("section") * lax.axis_size("tp")
    owners_each = max(1, ep_count // E)
    experts_each = max(1, E // ep_count)
    local_cols = gate_proj.shape[2]
    group_cols = local_cols * share_count
    owner_index = lax.axis_index("ep")
    share_index = lax.axis_index("section") * lax.axis_size("tp") + lax.axis_index("tp")
    own_expert = (owner_index * group_cols + share_index * local_cols) // F
    slot_expert = owner_index // owners_each * experts_each + jnp.arange(
        experts_each, dtype=jnp.int32
    )
    keep_mask = (slot_expert == own_expert).reshape(1, experts_each, 1, 1)
    gate_local = gate_proj[0]
    up_local = up_proj[0]
    down_local = down_proj[0]
    dispatch, slot_of = slot_tables(expert_ids, CAP, E)
    packed = jnp.dot(
        dispatch,
        lax.all_gather(hidden, ("section", "tp"), axis=1, tiled=True),
        preferred_element_type=jnp.float32,
    ).astype(jnp.bfloat16)
    grouped = packed.reshape(E // experts_each, experts_each, CAP, packed.shape[1])
    received = lax.all_to_all(
        jnp.repeat(grouped, owners_each, axis=0), "ep", split_axis=0, concat_axis=0, tiled=True
    )
    flat_rows = received.reshape(-1, received.shape[3])
    gate_out = jnp.dot(flat_rows, gate_local, preferred_element_type=jnp.float32)
    up_out = jnp.dot(flat_rows, up_local, preferred_element_type=jnp.float32)
    lead_shape = received.shape[:3]
    activated = (jax.nn.silu(gate_out) * up_out).reshape(lead_shape + (local_cols,))
    activated = jnp.where(keep_mask, activated, 0.0).astype(jnp.bfloat16)
    flat_act = activated.reshape(-1, local_cols)
    outputs = lax.dot_general(
        lax.all_gather(flat_act, ("section", "tp"), axis=1, tiled=True),
        down_local,
        (((1,), (1,)), ((), ())),
        preferred_element_type=jnp.float32,
    )
    outputs = outputs.reshape(lead_shape + (down_local.shape[0],)).astype(jnp.bfloat16)
    returned = lax.all_to_all(outputs, "ep", split_axis=0, concat_axis=0, tiled=True)
    grouped = returned.astype(jnp.float32).reshape(
        E // experts_each, owners_each, experts_each, CAP, returned.shape[3]
    )
    summed = jnp.sum(grouped, axis=1).reshape(E * CAP, returned.shape[3])
    first_rows = summed[slot_of[:, 0]]
    second_rows = summed[slot_of[:, 1]]
    combined_out = gate_weights[:, 0:1] * first_rows + gate_weights[:, 1:2] * second_rows
    return combined_out.astype(jnp.bfloat16)

SLOTS = 10
PARTS = 3
CHUNKS = 4
MESH = pl.DeviceIdType.MESH


def layer_kernel(
    hidden_ref, ids_ref, weights_ref, gate_ref, up_ref, down_ref, out_ref,
    picks, scales, sent, landed, across, x_all, w_buf, d_buf, acc, act_all, totals, back, ret,
    z_send, z_recv, s_send, s_recv, x_send, x_recv, a_send, a_recv, c_send, c_recv, r_send, r_recv, w_sem, d_sem,
):
    width = hidden_ref.shape[1]
    part = width // PARTS
    rows = 4 * CAP
    half = rows // 2
    tokens = hidden_ref.shape[0]
    order = (0, 3, 1, 2)
    units = 2 * PARTS
    cols = gate_ref.shape[2]
    chunk = cols // CHUNKS
    steps = 4 * units
    section = lax.axis_index("section")
    z = lax.axis_index("ep")
    tp = lax.axis_index("tp")
    tx, ty = tp % 2, tp // 2
    other = 1 - section

    def place(rel):
        return (ty + rel // 2) % 2 * 2 + (tx + rel % 2) % 2

    x_near, y_near, far = place(1), place(2), place(3)

    def weight_copies(step):
        rel, unit = step // units, step % units
        core = (section + unit % 2) % 2
        row = pl.multiple_of(((core * 4 + place(rel)) * PARTS + unit // 2) * part, part)
        slot = step % SLOTS
        return [
            pltpu.make_async_copy(ref.at[0, pl.ds(row, part), :], w_buf.at[slot, i], w_sem.at[slot, i])
            for i, ref in enumerate((gate_ref, up_ref))
        ]

    def down_copy(index):
        at = pl.multiple_of(index * chunk, chunk)
        return pltpu.make_async_copy(down_ref.at[0, :, pl.ds(at, chunk)], d_buf.at[index], d_sem.at[index])

    barrier = pltpu.get_barrier_semaphore()
    for d in range(1, 4):
        pl.semaphore_signal(barrier, inc=1, device_id={"ep": (z + d) % 4}, device_id_type=MESH)
    pl.semaphore_signal(barrier, inc=1, device_id={"section": other}, device_id_type=MESH)
    pl.semaphore_signal(barrier, inc=1, device_id={"tp": x_near}, device_id_type=MESH)
    pl.semaphore_signal(barrier, inc=1, device_id={"tp": y_near}, device_id_type=MESH)

    @pl.loop(0, SLOTS)
    def _(step):
        for copy in weight_copies(step):
            copy.start()

    experts = lax.broadcasted_iota(jnp.int32, (2 * E, tokens), 0)
    hot = [experts == ids_ref[k : k + 1, :] for k in range(2)]
    named = jnp.where(hot[0] | hot[1], 1.0, 0.0).astype(jnp.bfloat16)
    ahead = lax.broadcasted_iota(jnp.int32, (tokens, tokens), 0) < lax.broadcasted_iota(
        jnp.int32, (tokens, tokens), 1
    )
    earlier = jnp.dot(
        named, jnp.where(ahead, 1.0, 0.0).astype(jnp.bfloat16), preferred_element_type=jnp.float32
    )
    slots = lax.broadcasted_iota(jnp.int32, (E * CAP, tokens), 0).astype(jnp.float32)
    chosen = []
    for k in range(2):
        position = jnp.sum(jnp.where(hot[k], earlier, 0.0), axis=0, keepdims=True)
        slot = ids_ref[k : k + 1, :].astype(jnp.float32) * CAP + position
        chosen.append(jnp.where(slots == slot, 1.0, 0.0))
        picks[k] = chosen[k].astype(jnp.bfloat16)
    dispatch = (chosen[0] + chosen[1]).astype(jnp.bfloat16)
    packed = jnp.dot(dispatch, hidden_ref[...], preferred_element_type=jnp.float32)
    packed = packed.astype(jnp.bfloat16)
    for g in range(4):
        for h in range(PARTS):
            sent[g, h] = packed[g * 2 * CAP : (g + 1) * 2 * CAP, h * part : (h + 1) * part]
    pl.semaphore_wait(barrier, 6)

    def remote(src, dst, send, recv, target):
        return pltpu.make_async_remote_copy(
            src_ref=src, dst_ref=dst, send_sem=send, recv_sem=recv, device_id=target, device_id_type=MESH
        )

    def z_copy(h, d):
        g = (z + d) % 4
        return remote(sent.at[g, h], landed.at[z, h], z_send.at[h, g], z_recv.at[h, z], {"ep": g})

    def z_arrival(h, d):
        g = (z + d) % 4
        return remote(sent.at[g, h], landed.at[g, h], z_send.at[h, g], z_recv.at[h, g], {"ep": g})

    @pl.loop(0, PARTS)
    def _(h):
        for d in (2, 1, 3):
            z_copy(h, d).start()

    @pl.loop(0, 8 * CHUNKS)
    def _(index):
        down_copy(index).start()

    for h in range(PARTS):
        landed[z, h] = sent[z, h]
    for k in range(2):
        scales[k] = jnp.broadcast_to(weights_ref[k : k + 1, :], (tokens, tokens)).T
    acc[...] = jnp.zeros_like(acc)
    totals[...] = jnp.zeros_like(totals)

    def part_of(buf, index, kind):
        if buf is x_all:
            return buf.at[index, pl.ds((half, 0)[kind - 2], half), :]
        return buf.at[index, :, pl.ds((chunk // 2, 0)[kind - 2], chunk // 2)]

    def spread(buf, at, send, recv, kind, unit):
        if kind < 2:
            index, target = at(tp, unit), {"tp": (x_near, y_near)[kind]}
            ref = buf.at[index]
        else:
            index, target = at((x_near, y_near)[kind - 2], unit), {"tp": (y_near, x_near)[kind - 2]}
            ref = part_of(buf, index, kind)
        return remote(ref, ref, send.at[kind, unit], recv.at[kind, unit], target)

    def arrival(buf, at, send, recv, kind, unit):
        if kind < 2:
            ref = buf.at[at((x_near, y_near)[kind], unit)]
        else:
            ref = part_of(buf, at(far, unit), kind)
        return remote(ref, ref, send.at[kind, unit], recv.at[kind, unit], {"tp": (x_near, y_near, y_near, x_near)[kind]})

    def x_at(place_of, unit):
        return place_of * units + unit

    x_args = (x_all, x_at, x_send, x_recv)

    def swap_copy(h):
        return remote(
            across.at[h], x_all.at[x_at(tp, 2 * h + 1)], s_send.at[h], s_recv.at[h], {"section": other}
        )

    def gate_step(rel, unit):
        step = rel * units + unit
        slot = step % SLOTS
        for copy in weight_copies(step):
            copy.wait()
        x = x_all[x_at(place(rel), unit)]
        for i in range(2):
            for j in range(CHUNKS):
                acc[i, j] += jnp.dot(
                    x, w_buf[slot, i, :, j * chunk : (j + 1) * chunk], preferred_element_type=jnp.float32
                )

        @pl.when(step + SLOTS < steps)
        def _():
            for copy in weight_copies(step + SLOTS):
                copy.start()

    @pl.loop(0, PARTS)
    def _(h):
        for d in (1, 3, 2):
            z_arrival(h, d).wait_recv()
        blocks = [landed[g, h].astype(jnp.float32) for g in order]
        first = jnp.concatenate([b[:CAP] for b in blocks], axis=0)
        second = jnp.concatenate([b[CAP:] for b in blocks], axis=0)
        across[h] = jnp.where(section == 0, second, first).astype(jnp.bfloat16)
        swap_copy(h).start()
        x_all[x_at(tp, 2 * h)] = jnp.where(section == 0, first, second).astype(jnp.bfloat16)
        spread(*x_args, 0, 2 * h).start()
        spread(*x_args, 1, 2 * h).start()
        swap_copy(h).wait_recv()
        spread(*x_args, 0, 2 * h + 1).start()
        spread(*x_args, 1, 2 * h + 1).start()
        gate_step(0, 2 * h)
        gate_step(0, 2 * h + 1)

    @pl.loop(0, units)
    def _(unit):
        for kind in range(2):
            arrival(*x_args, kind, unit).wait_recv()
            spread(*x_args, kind + 2, unit).start()
        gate_step(1, unit)

    @pl.loop(0, units)
    def _(unit):
        gate_step(2, unit)

    @pl.loop(0, units)
    def _(unit):
        for kind in (2, 3):
            arrival(*x_args, kind, unit).wait_recv()
        gate_step(3, unit)

    def act_at(place_of, unit, core=None):
        return ((section if core is None else core) * 4 + place_of) * 2 * CHUNKS + unit

    a_args = (act_all, act_at, a_send, a_recv)

    def cross_copy(rel, unit):
        ref = act_all.at[act_at(place(rel), unit)]
        return remote(ref, ref, c_send.at[rel, unit], c_recv.at[rel, unit], {"section": other})

    def cross_arrival(rel, unit):
        ref = act_all.at[act_at(place(rel), unit, other)]
        return remote(ref, ref, c_send.at[rel, unit], c_recv.at[rel, unit], {"section": other})

    def down_step(core, rel, r, j):
        index = (core * 4 + place(rel)) * CHUNKS + j
        if r == 0:
            down_copy(index).wait()
        totals[core, r] += lax.dot_general(
            act_all[act_at(place(rel), r * CHUNKS + j, core)], d_buf[index], (((1,), (1,)), ((), ())),
            preferred_element_type=jnp.float32,
        )

    def activate(r, j):
        unit = r * CHUNKS + j
        gate_out = acc[0, j, r * half : (r + 1) * half]
        up_out = acc[1, j, r * half : (r + 1) * half]
        act_all[act_at(tp, unit)] = (gate_out / (1.0 + jnp.exp(-gate_out)) * up_out).astype(jnp.bfloat16)
        spread(*a_args, 0, unit).start()
        spread(*a_args, 1, unit).start()
        cross_copy(0, unit).start()

    def pass_on(unit):
        for kind in range(2):
            arrival(*a_args, kind, unit).wait_recv()
            spread(*a_args, kind + 2, unit).start()
            cross_copy(kind + 1, unit).start()

    def far_in(unit):
        for kind in (2, 3):
            arrival(*a_args, kind, unit).wait_recv()
        cross_copy(3, unit).start()

    def own_steps(r, j):
        down_step(section, 0, r, j)
        cross_arrival(0, r * CHUNKS + j).wait_recv()
        down_step(other, 0, r, j)

    def rest_steps(r, j):
        for rel in (1, 2):
            cross_arrival(rel, r * CHUNKS + j).wait_recv()
            down_step(other, rel, r, j)
        down_step(section, 3, r, j)

    def last_steps(r, j):
        cross_arrival(3, r * CHUNKS + j).wait_recv()
        down_step(other, 3, r, j)

    def back_copy(g):
        return remote(back.at[g], ret.at[z], r_send.at[g], r_recv.at[z], {"ep": g})

    def back_arrival(d):
        g = (z + d) % 4
        return remote(back.at[g], ret.at[g], r_send.at[g], r_recv.at[g], {"ep": g})

    def give_back(r):
        for i in range(2):
            g = order[2 * r + i]
            back[g] = jnp.concatenate(
                [totals[e, r, i * CAP : (i + 1) * CAP, :] for e in range(2)], axis=0
            ).astype(jnp.bfloat16)

            @pl.when(z != g)
            def _():
                back_copy(g).start()

            @pl.when(z == g)
            def _():
                ret[z] = back[g]

    @pl.loop(0, CHUNKS)
    def _(j):
        activate(0, j)

    @pl.loop(0, CHUNKS)
    def _(j):
        own_steps(0, j)
        pass_on(j)
        activate(1, j)

    @pl.loop(0, CHUNKS)
    def _(j):
        down_step(section, 1, 0, j)
        down_step(section, 2, 0, j)
        far_in(j)
        pass_on(CHUNKS + j)
        rest_steps(0, j)

    @pl.loop(0, CHUNKS)
    def _(j):
        last_steps(0, j)

    give_back(0)

    @pl.loop(0, CHUNKS)
    def _(j):
        own_steps(1, j)
        down_step(section, 1, 1, j)
        down_step(section, 2, 1, j)
        far_in(CHUNKS + j)
        rest_steps(1, j)

    @pl.loop(0, CHUNKS)
    def _(j):
        last_steps(1, j)

    give_back(1)
    for d in (1, 3, 2):
        back_arrival(d).wait_recv()
    flat = ret[...].reshape(8 * CAP, width)
    combined = 0.0
    for k in range(2):
        taken = lax.dot_general(picks[k], flat, (((0,), (0,)), ((), ())), preferred_element_type=jnp.float32)
        combined = combined + scales[k][:, 0:1] * taken
    out_ref[...] = combined.astype(out_ref.dtype)

    for g in range(4):
        @pl.when(z != g)
        def _():
            back_copy(g).wait_send()

    @pl.loop(0, PARTS)
    def _(h):
        for d in range(1, 4):
            z_copy(h, d).wait_send()
        swap_copy(h).wait_send()

    @pl.loop(0, units)
    def _(unit):
        for kind in range(4):
            spread(*x_args, kind, unit).wait_send()

    @pl.loop(0, 2 * CHUNKS)
    def _(j):
        for kind in range(4):
            spread(*a_args, kind, j).wait_send()
        for rel in range(4):
            cross_copy(rel, j).wait_send()


def on_device_paired(hidden, expert_ids, gate_weights, gate_proj, up_proj, down_proj):
    tokens, width = hidden.shape
    cols = gate_proj.shape[2]
    part, chunk, rows = width // PARTS, cols // CHUNKS, 4 * CAP
    vmem = pl.BlockSpec(memory_space=pltpu.VMEM)
    anywhere = pl.BlockSpec(memory_space=pl.ANY)
    sem = pltpu.SemaphoreType.DMA
    return pl.pallas_call(
        layer_kernel,
        out_shape=jax.ShapeDtypeStruct((tokens, width), jnp.bfloat16),
        in_specs=[vmem] * 3 + [anywhere] * 3,
        out_specs=vmem,
        scratch_shapes=[
            pltpu.VMEM((2, E * CAP, tokens), jnp.bfloat16),
            pltpu.VMEM((2, tokens, tokens), jnp.float32),
            pltpu.VMEM((4, PARTS, 2 * CAP, part), jnp.bfloat16),
            pltpu.VMEM((4, PARTS, 2 * CAP, part), jnp.bfloat16),
            pltpu.VMEM((PARTS, rows, part), jnp.bfloat16),
            pltpu.VMEM((8 * PARTS, rows, part), jnp.bfloat16),
            pltpu.VMEM((SLOTS, 2, part, cols), jnp.bfloat16),
            pltpu.VMEM((8 * CHUNKS, width, chunk), jnp.bfloat16),
            pltpu.VMEM((2, CHUNKS, rows, chunk), jnp.float32),
            pltpu.VMEM((16 * CHUNKS, rows // 2, chunk), jnp.bfloat16),
            pltpu.VMEM((2, 2, rows // 2, width), jnp.float32),
            pltpu.VMEM((4, 2 * CAP, width), jnp.bfloat16),
            pltpu.VMEM((4, 2 * CAP, width), jnp.bfloat16),
            sem((PARTS, 4)), sem((PARTS, 4)), sem((PARTS,)), sem((PARTS,)),
            sem((4, 2 * PARTS)), sem((4, 2 * PARTS)), sem((4, 2 * CHUNKS)), sem((4, 2 * CHUNKS)),
            sem((4, 2 * CHUNKS)), sem((4, 2 * CHUNKS)), sem((4,)), sem((4,)),
            sem((SLOTS, 2)), sem((8 * CHUNKS,)),
        ],
        compiler_params=pltpu.CompilerParams(
            collective_id=0, has_side_effects=True, vmem_limit_bytes=62 * 1024 * 1024
        ),
    )(hidden, expert_ids.T, gate_weights.T, gate_proj, up_proj, down_proj)


def solution(mesh):
    def body(*args):
        paired = mesh.shape["ep"] == 4 and mesh.shape["section"] == 2 and mesh.shape["tp"] == 4
        paired = paired and E // mesh.shape["ep"] == mesh.shape["section"] and args[3].shape[2] * mesh.shape["tp"] == F
        return (on_device_paired if paired else on_device)(*args)

    return jax.shard_map(
        body,
        mesh=mesh,
        in_specs=(
            P("ep", ("section", "tp")),
            P("ep", None),
            P("ep", None),
            P("ep", None, ("section", "tp")),
            P("ep", None, ("section", "tp")),
            P("ep", ("section", "tp"), None),
        ),
        out_specs=P("ep", ("section", "tp")),
        check_vma=False,
    )
```
